512 devices in a mesh: ctx: 16 (over x, z_hi), mem: 32 (over y, z_lo, core).
Axes of the slice: x: 4, y: 4, z: 16 (z_hi: 4, z_lo: 4; z = z_hi * 4 + z_lo), core: 2. Of those that a mesh axis runs over, the one named last changes fastest.
Arguments:
- queries: bfloat16 [6144, 4096], P('ctx', 'mem'), may hold values from -6 to 6
- keys: bfloat16 [6144, 4096], P('ctx', 'mem'), may hold values from -6 to 6
- values: bfloat16 [6144, 4096], P('ctx', 'mem'), may hold values from -6 to 6
- out_grad: bfloat16 [6144, 4096], P('ctx', 'mem'), may hold values from -6 to 6
- mem_keys: bfloat16 [4096, 4096], P('mem'), may hold values from -6 to 6
- mem_values: bfloat16 [4096, 4096], P('mem'), may hold values from -6 to 6
- gate_logit: float32 [32], P('mem'), may hold values from -3 to 3
- block_ids: int32 [48, 4], P('ctx'), may hold values from 0 to 31, all different within a row
Outputs:
- mixed: bfloat16 [6144, 4096], P('ctx', 'mem')
- query_grad: bfloat16 [6144, 4096], P('ctx', 'mem')
- mem_key_grad: bfloat16 [4096, 4096], P('mem', 'ctx')
- mem_value_grad: bfloat16 [4096, 4096], P('mem', 'ctx')
The draws below stay inside these ranges and needn't reach their ends.
Inputs may be any that keep to these rules, and one draw needn't show every extreme that they name: `block_ids`: the 4 ids listed for one query block are distinct, and every memory block is listed somewhere.
All inputs are finite; a program needn't handle non-finite values.
Results may differ from the reference program's by a relative error of at most 0.02.
Values may be sent and summed in bfloat16 or wider, within the bound.
No kernel may reach another device: no remote copies, remote signals or barrier semaphores. Data moves between devices by JAX's collectives and lax.ppermute only.
A program may use at most 64 MiB of HBM per device.

```python
import jax
import jax.numpy as jnp
from jax import lax

HEADS = 32
HEAD_SIZE = 128
D = 4096
BLOCK = 128
LIST = 4
TOK_DEV = 384
SEQUENCE_TOKENS = 6144
NQB = 48
MEM_BLOCKS = 32
MEM_ROWS = 4096
N_CTX = 16


def draw_queries(key, part):
    drawn = jnp.clip(jax.random.normal(jax.random.fold_in(key, 11), (SEQUENCE_TOKENS, D), jnp.float32), -6.0, 6.0)
    return drawn.astype(jnp.bfloat16)


def draw_keys(key, part):
    drawn = jnp.clip(jax.random.normal(jax.random.fold_in(key, 12), (SEQUENCE_TOKENS, D), jnp.float32), -6.0, 6.0)
    return drawn.astype(jnp.bfloat16)


def draw_mem_keys(key, part):
    drawn = jnp.clip(jax.random.normal(jax.random.fold_in(key, 13), (MEM_ROWS, D), jnp.float32), -6.0, 6.0)
    return drawn.astype(jnp.bfloat16)


def levels(rng, extent, cuts, low, top_value):
    factor_of = 1.0
    for position, blocks in cuts:
        draws = jax.random.uniform(jax.random.fold_in(jax.random.fold_in(rng, 6), position), (blocks,), jnp.float32, low / len(cuts), top_value / len(cuts))
        factor_of = factor_of * jnp.repeat(jnp.exp(draws), extent[position] // blocks).reshape((-1,) + (1,) * (len(extent) - 1 - position))
    return factor_of


def different_ones(own_key, rows, count, top, lift):
    order = jax.random.permutation(jax.random.fold_in(own_key, 1), count)
    favour = order
    for power in range(3):
        favour = favour * favour // count
    favour = favour * lift // count
    chance = jax.random.randint(jax.random.fold_in(own_key, 2), (rows, count), 0, 4096) + favour
    sure = jax.random.permutation(jax.random.fold_in(own_key, 3), rows)[jnp.arange(count) % rows]
    chance = jnp.where(jnp.arange(rows)[:, None] == sure[None, :], 1 << 14, chance)
    score = chance * count + jnp.arange(count)
    return lax.top_k(score.astype(jnp.int32), top)[1].astype(jnp.int32)


def centred(key, shape, spread, most, cuts=(), kind=jnp.bfloat16):
    values = jax.random.normal(key, shape, jnp.float32) * spread
    if len(cuts) > 0:
        values = levels(key, shape, cuts, -0.22, 0.18) * values
    return jnp.clip(values, min=-most, max=most).astype(kind)


def setup_inputs(seed: int = 0) -> dict:
    streams_of = jax.random.split(jax.random.key(seed), 9)
    return {
        "queries": draw_queries(jax.random.fold_in(streams_of[8], 71), 0),
        "keys": draw_keys(jax.random.fold_in(streams_of[8], 71), 0),
        "values": centred(streams_of[2], (SEQUENCE_TOKENS, D), 1.0, 6.0, ((0, 16), (1, 32))),
        "out_grad": centred(streams_of[3], (SEQUENCE_TOKENS, D), 1.0, 6.0, ((0, 16), (1, 32))),
        "mem_keys": draw_mem_keys(jax.random.fold_in(streams_of[8], 71), 0),
        "mem_values": centred(streams_of[5], (MEM_ROWS, D), 1.0, 6.0, ((0, 32),)),
        "gate_logit": jnp.clip(jax.random.uniform(streams_of[6], (HEADS,), jnp.float32, -3.0, 3.0) * levels(streams_of[6], (HEADS,), ((0, 32),), -0.4, 0.0), -3.0, 3.0),
        "block_ids": different_ones(streams_of[7], NQB, MEM_BLOCKS, LIST, 2048),
    }


def rounded(array):
    return lax.optimization_barrier(array.astype(jnp.bfloat16)).astype(jnp.float32)


def head_pass(inputs, block_ids):
    query, key_rows, value_rows, grad_rows, memory_keys, memory_values, gate_share = inputs
    scores_scale_factor = HEAD_SIZE ** -0.5
    positions = jnp.arange(SEQUENCE_TOKENS)
    causal = positions[None, :] <= positions[:, None]
    scores = jnp.dot(query, key_rows.T, preferred_element_type=jnp.float32) * scores_scale_factor
    masked = jnp.where(causal, scores, -1e30)
    row_max = jnp.max(masked, axis=-1)
    exp_terms = jnp.where(causal, jnp.exp(masked - row_max[:, None]), 0.0)
    row_total = jnp.sum(exp_terms, axis=-1)
    local_out = jnp.dot(exp_terms.astype(jnp.bfloat16), value_rows, preferred_element_type=jnp.float32) / row_total[:, None]
    log_total = row_max + jnp.log(row_total)

    query_block_list = query.reshape(NQB, BLOCK, HEAD_SIZE).astype(jnp.float32)
    selected_keys = memory_keys.reshape(MEM_BLOCKS, BLOCK, HEAD_SIZE)[block_ids].reshape(NQB, LIST * BLOCK, HEAD_SIZE).astype(jnp.float32)
    selected_values = memory_values.reshape(MEM_BLOCKS, BLOCK, HEAD_SIZE)[block_ids].reshape(NQB, LIST * BLOCK, HEAD_SIZE).astype(jnp.float32)
    memory_score_matrix = jnp.einsum("iom,ipm->iop", query_block_list, selected_keys) * scores_scale_factor
    weights = jax.nn.softmax(memory_score_matrix, axis=-1)
    weights_reduced = rounded(weights)
    memory_output = jnp.einsum("plz,pzr->plr", weights_reduced, selected_values).reshape(SEQUENCE_TOKENS, HEAD_SIZE)
    mixed = (gate_share * memory_output + (1.0 - gate_share) * local_out).astype(jnp.bfloat16)

    grad_full = grad_rows.astype(jnp.float32)
    grad_mem = gate_share * grad_full
    grad_local = (1.0 - gate_share) * grad_full
    probs = jnp.where(causal, jnp.exp(masked - log_total[:, None]), 0.0)
    grad_probs = jnp.dot(grad_local.astype(jnp.bfloat16), value_rows.T, preferred_element_type=jnp.float32)
    local_delta = jnp.sum(grad_local * local_out, axis=-1)
    grad_scores = probs * (grad_probs - local_delta[:, None])
    local_grad = jnp.dot(grad_scores.astype(jnp.bfloat16), key_rows, preferred_element_type=jnp.float32) * scores_scale_factor

    memory_gradient_reduced = rounded(grad_mem).reshape(NQB, BLOCK, HEAD_SIZE)
    weight_gradient = jnp.einsum("iom,ipm->iop", memory_gradient_reduced, selected_values)
    mem_delta = jnp.sum(grad_mem * memory_output, axis=-1).reshape(NQB, BLOCK)
    memory_score_gradient = rounded(weights * (weight_gradient - mem_delta[:, :, None]))
    memory_gradient = jnp.einsum("plz,pzr->plr", memory_score_gradient, selected_keys).reshape(SEQUENCE_TOKENS, HEAD_SIZE) * scores_scale_factor
    selected_key_gradient = jnp.einsum("spn,spu->snu", memory_score_gradient, query_block_list) * scores_scale_factor
    selected_value_gradient = jnp.einsum("spn,spu->snu", weights_reduced, memory_gradient_reduced)
    query_grad = (memory_gradient + local_grad).astype(jnp.bfloat16)

    per_segment = TOK_DEV // BLOCK * LIST
    seg_keys = selected_key_gradient.reshape(N_CTX, per_segment, BLOCK, HEAD_SIZE)
    seg_values = selected_value_gradient.reshape(N_CTX, per_segment, BLOCK, HEAD_SIZE)
    seg_ids = block_ids.reshape(N_CTX, per_segment)
    block_numbers = jnp.arange(MEM_BLOCKS).astype(jnp.int32)

    def add_segment(totals, pieces):
        piece_keys, piece_values, piece_ids = pieces
        one_hot = (piece_ids[:, None] == block_numbers[None, :]).astype(jnp.float32)
        part_keys = jnp.einsum("jb,jrd->brd", one_hot, piece_keys, precision=lax.Precision.HIGHEST)
        part_values = jnp.einsum("jb,jrd->brd", one_hot, piece_values, precision=lax.Precision.HIGHEST)
        return (totals[0] + rounded(part_keys), totals[1] + rounded(part_values)), None

    empty = jnp.zeros((MEM_BLOCKS, BLOCK, HEAD_SIZE), jnp.float32)
    (key_total, value_total), _ = lax.scan(add_segment, (empty, empty), (seg_keys, seg_values, seg_ids))
    return (mixed, query_grad, key_total.reshape(MEM_ROWS, HEAD_SIZE).astype(jnp.bfloat16),
            value_total.reshape(MEM_ROWS, HEAD_SIZE).astype(jnp.bfloat16))


def heads_first(array, row_count):
    return array.reshape(row_count, HEADS, HEAD_SIZE).transpose(1, 0, 2)


def rows_first(array, row_count):
    return array.transpose(1, 0, 2).reshape(row_count, D)


def reference(queries, keys, values, out_grad, mem_keys, mem_values, gate_logit, block_ids):
    gate_values = jax.nn.sigmoid(gate_logit.astype(jnp.float32))
    stacked = (heads_first(queries, SEQUENCE_TOKENS), heads_first(keys, SEQUENCE_TOKENS), heads_first(values, SEQUENCE_TOKENS),
               heads_first(out_grad, SEQUENCE_TOKENS), heads_first(mem_keys, MEM_ROWS), heads_first(mem_values, MEM_ROWS),
               gate_values)
    mixed, query_grad, key_grad, value_grad = lax.map(lambda inputs: head_pass(inputs, block_ids), stacked)
    return (rows_first(mixed, SEQUENCE_TOKENS), rows_first(query_grad, SEQUENCE_TOKENS),
            rows_first(key_grad, MEM_ROWS), rows_first(value_grad, MEM_ROWS))
```

```python
import jax
import jax.numpy as jnp
from jax import lax
from jax.experimental import pallas as pl
from jax.experimental.pallas import tpu as pltpu
from jax.sharding import Mesh, PartitionSpec as P

HEAD = 128
BLOCK = 128
SEG = 384
QB = 3
LIST = 4
NX = 4
NZ = 4
NBLK = 32
PART = BLOCK // NX
SCALE = HEAD ** -0.5
EXPC = SCALE * 1.4426950408889634
NEG = -1e30
F32 = jnp.float32
BF = jnp.bfloat16
VM = pl.BlockSpec(memory_space=pltpu.VMEM)
SM = pl.BlockSpec(memory_space=pltpu.SMEM)


def nt(a, b):
    return lax.dot_general(a, b, (((1,), (1,)), ((), ())), preferred_element_type=F32)


def nn(a, b):
    return lax.dot_general(a, b, (((1,), (0,)), ((), ())), preferred_element_type=F32)


def tn(a, b):
    return lax.dot_general(a, b, (((0,), (0,)), ((), ())), preferred_element_type=F32)


def split3(row):
    first = row.astype(BF)
    rest = row - first.astype(F32)
    second = rest.astype(BF)
    third = (rest - second.astype(F32)).astype(BF)
    return [first, second, third]


def gathered(mem_ref, ids_ref, block, lo):
    return jnp.concatenate(
        [mem_ref[ids_ref[block, j], lo : lo + PART, :] for j in range(LIST)], axis=0
    )


def mem_forward(ids_ref, gate_ref, qd_ref, mem_ref, e_ref, dw_ref, stat_ref):
    gate = gate_ref[0]
    for block in range(NX * QB):
        seg, b = block // QB, block % QB
        query = qd_ref[seg, b * BLOCK : (b + 1) * BLOCK, :]
        grad = qd_ref[seg, SEG + b * BLOCK : SEG + (b + 1) * BLOCK, :]
        dm = (gate * grad.astype(F32)).astype(BF)
        keys = gathered(mem_ref, ids_ref, block, 0)
        vals = gathered(mem_ref, ids_ref, block, PART)
        scores = nt(keys, query)
        top = jnp.max(scores, axis=0, keepdims=True)
        e = jnp.exp2((scores - top) * EXPC)
        dw = nt(vals, dm)
        e_ref[block] = e
        dw_ref[block] = dw
        stat_ref[0, block : block + 1, :] = top
        stat_ref[1, block : block + 1, :] = jnp.sum(e, axis=0, keepdims=True)
        stat_ref[2, block : block + 1, :] = jnp.sum(e * dw, axis=0, keepdims=True)


def mem_backward(
    ids_ref, gate_ref, pos_ref, qd_ref, mem_ref, e_ref, dw_ref, s0, s1, s2, s3,
    part_ref, o0, o1, o2, o3, grads,
):
    gate = gate_ref[0]
    zh = pos_ref[1]
    grads[...] = jnp.zeros_like(grads)
    stats = (s0, s1, s2, s3)
    top = jnp.maximum(jnp.maximum(s0[0], s1[0]), jnp.maximum(s2[0], s3[0]))
    shares = [jnp.exp2((s[0] - top) * EXPC) for s in stats]
    total = sum(w * s[1] for w, s in zip(shares, stats))
    delta = sum(w * s[2] for w, s in zip(shares, stats)) / total
    factor = shares[0] / total
    for block in range(NX * QB):
        seg, b = block // QB, block % QB
        query = qd_ref[seg, b * BLOCK : (b + 1) * BLOCK, :]
        grad = qd_ref[seg, SEG + b * BLOCK : SEG + (b + 1) * BLOCK, :]
        dm = (gate * grad.astype(F32)).astype(BF)
        keys = gathered(mem_ref, ids_ref, block, 0)
        vals = gathered(mem_ref, ids_ref, block, PART)
        w = e_ref[block] * factor[block : block + 1, :]
        wb = w.astype(BF)
        dmat = (w * (dw_ref[block] - delta[block : block + 1, :])).astype(BF)
        cols = slice(b * BLOCK, (b + 1) * BLOCK)
        part_ref[seg, 0:HEAD, cols] = (gate * tn(vals, wb)).astype(BF)
        part_ref[seg, HEAD : 2 * HEAD, cols] = (SCALE * tn(keys, dmat)).astype(BF)
        dk = nn(dmat, query) * SCALE
        dv = nn(wb, dm)
        for j in range(LIST):
            rows = slice(j * PART, (j + 1) * PART)
            which = ids_ref[block, j]
            grads[which, 0:PART, :] += dk[rows]
            grads[which, PART : 2 * PART, :] += dv[rows]
    for j, out in enumerate((o0, o1, o2, o3)):
        z = lax.rem(zh + j, NZ)
        for y in range(4):
            for core in range(2):
                out[y * 2 + core] = grads[y * 8 + z * 2 + core].astype(BF)


def local_kernel(
    gate_ref, pos_ref, qd_ref, k0, k1, k2, k3, v0, v1, v2, v3, out_ref, s_ref, vk_ref, acc_ref, row_ref
):
    x = pos_ref[0]
    zh = pos_ref[1]
    rest = 1.0 - gate_ref[0]
    keys = (k0, k1, k2, k3)
    vals = (v0, v1, v2, v3)
    for p in range(NZ):
        vk_ref[p, 0:HEAD, :] = vals[p][...].T
        vk_ref[p, HEAD : 2 * HEAD, :] = keys[p][...].T

    @pl.loop(0, NX)
    def _(xp):
        @pl.when(xp < x)
        def _():
            out_ref[xp] = jnp.zeros((3 * HEAD + 16, SEG), BF)
            out_ref[xp, 3 * HEAD : 3 * HEAD + 1, :] = jnp.full((1, SEG), NEG, BF)

        @pl.when(xp >= x)
        def _():
            query = qd_ref[xp, 0:SEG, :]
            grad = qd_ref[xp, SEG : 2 * SEG, :]
            dl = (rest * grad.astype(F32)).astype(BF)
            row_ref[...] = jnp.full((8, SEG), NEG, F32)
            later = xp > x
            for p in range(NZ):
                seg = lax.rem(zh + NZ - p, NZ)

                @pl.when(jnp.logical_or(later, seg <= zh))
                def _():
                    scores = nt(keys[p][...], query)
                    if p == 0:
                        krow = lax.broadcasted_iota(jnp.int32, (SEG, SEG), 0)
                        qcol = lax.broadcasted_iota(jnp.int32, (SEG, SEG), 1)
                        slack = jnp.where(later, SEG, 0)
                        scores = jnp.where(krow <= qcol + slack, scores, NEG)
                    s_ref[p] = scores
                    row_ref[0:1, :] = jnp.maximum(row_ref[0:1, :], jnp.max(scores, axis=0, keepdims=True))

            top = row_ref[0:1, :]
            row_ref[1:3, :] = jnp.zeros((2, SEG), F32)
            acc_ref[...] = jnp.zeros_like(acc_ref)
            for p in range(NZ):
                seg = lax.rem(zh + NZ - p, NZ)

                @pl.when(jnp.logical_or(later, seg <= zh))
                def _():
                    e = jnp.exp2((s_ref[p] - top) * EXPC)
                    ed = e * nt(vals[p][...], dl)
                    row_ref[1:2, :] += jnp.sum(e, axis=0, keepdims=True)
                    row_ref[2:3, :] += jnp.sum(ed, axis=0, keepdims=True)
                    acc_ref[0 : 2 * HEAD, :] += nn(vk_ref[p], e.astype(BF))
                    acc_ref[2 * HEAD : 3 * HEAD, :] += nn(vk_ref[p, HEAD : 2 * HEAD, :], ed.astype(BF))

            out_ref[xp, 0 : 3 * HEAD, :] = acc_ref[...].astype(BF)
            rows = split3(top) + split3(row_ref[1:2, :]) + split3(row_ref[2:3, :])
            rows = [r.astype(F32) for r in rows] + [jnp.zeros((7, SEG), F32)]
            out_ref[xp, 3 * HEAD : 3 * HEAD + 16, :] = jnp.concatenate(rows, axis=0).astype(BF)


def final_kernel(gate_ref, loc_ref, mem_ref, mixed_ref, dq_ref):
    rest = 1.0 - gate_ref[0]

    def stat(i, n):
        rows = loc_ref[i, 3 * HEAD : 3 * HEAD + 16, :].astype(F32)
        return rows[3 * n : 3 * n + 1] + rows[3 * n + 1 : 3 * n + 2] + rows[3 * n + 2 : 3 * n + 3]

    tops = [stat(i, 0) for i in range(NX)]
    top = jnp.maximum(jnp.maximum(tops[0], tops[1]), jnp.maximum(tops[2], tops[3]))
    shares = [jnp.exp2((t - top) * EXPC) for t in tops]
    total = sum(w * stat(i, 1) for i, w in enumerate(shares))
    delta = sum(w * stat(i, 2) for i, w in enumerate(shares)) / total
    factors = [w / total for w in shares]

    def weighted(lo):
        return sum(f * loc_ref[i, lo : lo + HEAD, :].astype(F32) for i, f in enumerate(factors))

    def memory(lo):
        return sum(mem_ref[i, lo : lo + HEAD, :].astype(F32) for i in range(NX))

    mixed = memory(0) + rest * weighted(0)
    dq = memory(HEAD) + SCALE * (weighted(2 * HEAD) - delta * weighted(HEAD))
    mixed_ref[...] = mixed.T.astype(BF)
    dq_ref[...] = dq.T.astype(BF)


def shift(n, by):
    return [(i, (i + by) % n) for i in range(n)]


def shards(queries, keys, values, out_grad, mem_keys, mem_values, gate_logit, block_ids):
    x = lax.axis_index("x")
    zh = lax.axis_index("zh")
    pos = jnp.stack([x, zh]).astype(jnp.int32)
    gate = jax.nn.sigmoid(gate_logit)

    ids_rows = jnp.zeros((16, HEAD), BF).at[0:QB, 0:LIST].set(block_ids.astype(BF))
    packed = jnp.concatenate([queries, out_grad, ids_rows], axis=0)
    qd = lax.all_to_all(jnp.broadcast_to(packed[None], (NX,) + packed.shape), "x", 0, 0)
    ids = qd[:, 2 * SEG : 2 * SEG + QB, 0:LIST].astype(jnp.int32).reshape(NX * QB, LIST)

    mine = jnp.concatenate(
        [
            lax.dynamic_slice_in_dim(mem_keys, x * PART, PART, 0),
            lax.dynamic_slice_in_dim(mem_values, x * PART, PART, 0),
        ],
        axis=0,
    )
    mine = mine.reshape(2 * PART, NBLK, HEAD).transpose(1, 0, 2)
    mem = lax.all_to_all(mine, ("y", "zl", "core"), 0, 0)

    k1 = lax.ppermute(keys, "zh", shift(NZ, 1))
    v3 = lax.ppermute(values, "zh", shift(NZ, -1))
    k3 = lax.ppermute(keys, "zh", shift(NZ, -1))
    v1 = lax.ppermute(values, "zh", shift(NZ, 1))
    k2 = lax.ppermute(k1, "zh", shift(NZ, 1))
    v2 = lax.ppermute(v3, "zh", shift(NZ, -1))

    nq = NX * QB
    e, dw, stat = pl.pallas_call(
        mem_forward,
        out_shape=(
            jax.ShapeDtypeStruct((nq, BLOCK, BLOCK), F32),
            jax.ShapeDtypeStruct((nq, BLOCK, BLOCK), F32),
            jax.ShapeDtypeStruct((3, nq, BLOCK), F32),
        ),
        in_specs=[SM, SM, VM, VM],
        out_specs=(VM, VM, VM),
        name="mem_fwd",
    )(ids, gate, qd, mem)
    others = [lax.ppermute(stat, "x", shift(NX, d)) for d in (1, 2, 3)]

    piece = jax.ShapeDtypeStruct((8, 2 * PART, HEAD), BF)
    part, *pieces = pl.pallas_call(
        mem_backward,
        out_shape=(jax.ShapeDtypeStruct((NX, 2 * HEAD, SEG), BF), piece, piece, piece, piece),
        in_specs=[SM, SM, SM] + [VM] * 8,
        out_specs=(VM,) * 5,
        scratch_shapes=[pltpu.VMEM((NBLK, 2 * PART, HEAD), F32)],
        name="mem_bwd",
    )(ids, gate, pos, qd, mem, e, dw, stat, *others)
    mem_part = lax.all_to_all(part, "x", 0, 0)

    got = [
        lax.ppermute(
            pieces[j],
            ("zh", "zl"),
            [(a * 4 + b, b * 4 + (a + j) % 4) for a in range(4) for b in range(4)],
        )
        for j in range(4)
    ]
    summed = sum(g.astype(F32) for g in got).astype(BF)
    swapped = lax.ppermute(summed, ("x", "y"), [(a * 4 + b, b * 4 + a) for a in range(4) for b in range(4)])
    landed = lax.all_to_all(swapped, ("y", "core"), 0, 0)
    landed = landed.reshape(4, 2, 2, PART, HEAD).transpose(2, 0, 3, 1, 4).reshape(2, BLOCK, 2 * HEAD)

    loc = pl.pallas_call(
        local_kernel,
        out_shape=jax.ShapeDtypeStruct((NX, 3 * HEAD + 16, SEG), BF),
        in_specs=[SM, SM] + [VM] * 9,
        out_specs=VM,
        scratch_shapes=[
            pltpu.VMEM((NZ, SEG, SEG), F32),
            pltpu.VMEM((NZ, 2 * HEAD, SEG), BF),
            pltpu.VMEM((3 * HEAD, SEG), F32),
            pltpu.VMEM((8, SEG), F32),
        ],
        name="local",
    )(gate, pos, qd, keys, k1, k2, k3, values, v1, v2, v3)
    loc_part = lax.all_to_all(loc, "x", 0, 0)

    mixed, dq = pl.pallas_call(
        final_kernel,
        out_shape=(jax.ShapeDtypeStruct((SEG, HEAD), BF),) * 2,
        in_specs=[SM, VM, VM],
        out_specs=(VM, VM),
        name="final",
    )(gate, loc_part, mem_part)
    return mixed, dq, landed[0], landed[1]


def solution(mesh):
    grid = Mesh(mesh.devices.reshape(4, 4, 4, 4, 2), ("x", "zh", "y", "zl", "core"))
    ctx, mem = ("x", "zh"), ("y", "zl", "core")
    in_specs = (P(ctx, mem),) * 4 + (P(mem, None),) * 2 + (P(mem), P(ctx, None))
    out_specs = (P(ctx, mem), P(ctx, mem), P(mem, ctx), P(mem, ctx))
    return jax.shard_map(shards, mesh=grid, in_specs=in_specs, out_specs=out_specs, check_vma=False)
```
